32 devices in a mesh: dp: 2 (over core), seq: 16 (over z, y, x).
Axes of the slice: x: 2, y: 2, z: 4, core: 2. Of those that a mesh axis runs over, the one named last changes fastest.
Arguments:
- loaded: bfloat16 [8192, 1024], P(('dp', 'seq')), may hold values from -6 to 6
- plan: int32 [32, 32], replicated, may hold values from 4 to 16, as said below
- segment_ids: int32 [4, 2048], P('dp'), may hold values from 0 to 31, never falling along the last dimension, each value on 1 to 1024 neighbouring positions
- in_weight: bfloat16 [1024, 2048], P('dp'), may hold values from -0.1875 to 0.1875
- out_weight: bfloat16 [1024, 1024], P('dp'), may hold values from -0.1875 to 0.1875
- depth_kernel: bfloat16 [1024, 31], P('dp'), may hold values from -2 to 2
- norm_gains: bfloat16 [1024, 2], P('dp'), may hold values from 0.25 to 1.75
- upstream: bfloat16 [4, 2048, 1024], P('dp', 'seq'), may hold values from -6 to 6
Outputs:
- encoded: bfloat16 [4, 2048, 1024], P('dp', 'seq')
- grad_frames: bfloat16 [4, 2048, 1024], P('dp', 'seq')
- grad_in_weight: float32 [1024, 2048], P('dp')
- grad_out_weight: float32 [1024, 1024], P('dp')
- grad_kernel: float32 [1024, 31], P('dp')
- grad_gains: float32 [1024, 2], P('dp')
The draws below stay inside these ranges and needn't reach their ends.
Inputs may be any that keep to these rules, and one draw needn't show every extreme that they name: Every row and every column of plan sums to 256; every row reaches 16.
All inputs are finite; a program needn't handle non-finite values.
Results may differ from the reference program's by a relative error of at most 0.006.
Values may be sent and summed in bfloat16 or wider, within the bound.
A program may use at most 128 MiB of HBM per device.

```python
import math
import jax
import jax.numpy as jnp
import numpy as np
from jax import lax

D = 1024
KERNEL = 31
SLAB_DEV = 128
SLABS = 2
SLAB = 2048
SLABS_ALL = 4
ROWS_DEV = 256
FRAMES_ALL = 8192
N_DP = 2
N_SEQ = 16
DEVICES = 32


def one_hot_rows(targets, count):
    columns = jnp.arange(count, dtype=jnp.int32)
    return (columns[None, :] == targets[:, None]).astype(jnp.int32)


def draw_plan(key, part):
    key_order = jax.random.fold_in(key, 11)
    key_near = jax.random.fold_in(key, 12)
    key_far = jax.random.fold_in(key, 13)
    ordering = jax.random.permutation(key_order, DEVICES).astype(jnp.int32)
    near_shift = jax.random.randint(key_near, (), 1, DEVICES // 2, dtype=jnp.int32)
    far_shift = jax.random.randint(key_far, (), DEVICES // 2, DEVICES, dtype=jnp.int32)
    sources = jnp.arange(DEVICES, dtype=jnp.int32)
    peak_cols = ordering[sources]
    near_cols = ordering[(sources + near_shift) % DEVICES]
    far_cols = ordering[(sources + far_shift) % DEVICES]
    halfway = ROWS_DEV // DEVICES // 2
    moved = 2 * one_hot_rows(peak_cols, DEVICES) - one_hot_rows(near_cols, DEVICES) - one_hot_rows(far_cols, DEVICES)
    return (2 * halfway + halfway * moved).astype(jnp.int32)


def levels(key, dims, split, least, high):
    level, own = 1.0, jax.random.fold_in(key, 6)
    for axis_at, parts in split:
        steps = jnp.exp(jax.random.uniform(jax.random.fold_in(own, axis_at), (parts,), jnp.float32, least / len(split), high / len(split)))
        level = level * jnp.repeat(steps, dims[axis_at] // parts).reshape([-1 if axis == axis_at else 1 for axis in range(len(dims))])
    return level


def split_up(amount, total, limit, lean):
    weights = [(1 << 20) // math.isqrt(rank ** lean) + 1 for rank in range(2, amount + 1)]
    rest, holding = total - limit - (amount - 1), [1] * (amount - 1)
    while rest > 0:
        free = [i for i in range(amount - 1) if holding[i] < limit]
        pool, left = sum([weights[i] for i in free]), rest
        for i in free:
            extra = min(limit - holding[i], max(1, left * weights[i] // pool), rest)
            holding[i] = holding[i] + extra
            rest = rest - extra
    return np.array([limit] + holding)


def ragged(rng, amount, total, reach, skew):
    if amount == 2:
        one = jax.random.randint(rng, (), max(1, total - reach), min(reach, total - 1) + 1)
        return jnp.stack([one, total - one])
    sizes = jnp.asarray(split_up(amount, total, reach, skew), jnp.int32)
    couples = (amount - 1) // 2
    donor, receiver = sizes[1:1 + 2 * couples:2], sizes[2:2 + 2 * couples:2]
    room = jnp.minimum(donor - 1, reach - receiver)
    shifted = jax.random.randint(jax.random.fold_in(rng, 1), (couples,), 0, 1 << 20) % (room + 1)
    sizes = sizes.at[1:1 + 2 * couples:2].set(donor - shifted).at[2:2 + 2 * couples:2].set(receiver + shifted)
    return sizes[jax.random.permutation(jax.random.fold_in(rng, 2), amount)]


def gaussian(stream_key, extent, deviation, bound, shards=(), kind=jnp.bfloat16):
    entries = jax.random.normal(stream_key, extent, jnp.float32) * deviation
    if len(shards) > 0:
        entries = levels(stream_key, extent, shards, -0.22, 0.18) * entries
    return jnp.clip(entries, min=-bound, max=bound).astype(kind)


def setup_inputs(seed: int = 0) -> dict:
    key_list = jax.random.split(jax.random.key(seed), 9)
    return {
        "loaded": gaussian(key_list[0], (DEVICES * ROWS_DEV, D), 1.0, 6.0, ((0, 32),)),
        "plan": draw_plan(jax.random.fold_in(key_list[8], 71), 0),
        "segment_ids": jax.vmap(lambda own: jnp.searchsorted(jnp.cumsum(ragged(own, SLAB // 64, SLAB, SLAB // 2, 2)), jnp.arange(SLAB), side="right"))(jax.random.split(key_list[2], SLABS_ALL)).reshape((SLABS_ALL, SLAB)).astype(jnp.int32),
        "in_weight": gaussian(key_list[3], (D, 2 * D), D ** -0.5, 0.1875, ((0, 2),)),
        "out_weight": gaussian(key_list[4], (D, D), D ** -0.5, 0.1875, ((0, 2),)),
        "depth_kernel": gaussian(key_list[5], (D, KERNEL), (KERNEL // 4) ** -0.5, 2.0, ((0, 2),)),
        "norm_gains": jnp.clip(1.0 + 0.15 * jax.random.normal(key_list[6], (D, 2), jnp.float32), 0.25, 1.75).astype(jnp.bfloat16),
        "upstream": gaussian(key_list[7], (SLABS_ALL, SLAB, D), 1.0, 6.0, ((0, 2), (1, 16))),
    }


def norm_rows(values, gain):
    average = lax.optimization_barrier(jnp.mean(values, axis=-1, keepdims=True))
    centered = values - average
    spread = lax.optimization_barrier(jnp.mean(centered * centered, axis=-1, keepdims=True))
    return centered * lax.rsqrt(spread + 1e-05) * gain

def mid_section(values, gain):
    normed = norm_rows(values, gain)
    return normed * jax.nn.sigmoid(normed)

def repack(loaded, plan):
    send_end = jnp.cumsum(plan, axis=1).astype(jnp.int32)
    send_start = (send_end - plan).astype(jnp.int32)
    recv_start = (jnp.cumsum(plan, axis=0) - plan).astype(jnp.int32)
    row_index = jnp.arange(ROWS_DEV, dtype=jnp.int32)
    target_dev = lax.optimization_barrier(jnp.sum((send_end[:, None, :] <= row_index[None, :, None]).astype(jnp.int32), axis=2)).astype(jnp.int32)
    source_dev = jnp.broadcast_to(jnp.arange(DEVICES, dtype=jnp.int32)[:, None], target_dev.shape)
    within = row_index[None, :] - send_start[source_dev, target_dev]
    target = (target_dev * ROWS_DEV + recv_start[source_dev, target_dev] + within).astype(jnp.int32)
    placed = jnp.zeros_like(loaded).at[target.reshape(-1)].set(loaded)
    grid = placed.reshape(N_DP, N_SEQ, SLABS, SLAB_DEV, D)
    return jnp.transpose(grid, (0, 2, 1, 3, 4)).reshape(SLABS_ALL, SLAB, D)

def reference(loaded, plan, segment_ids, in_weight, out_weight, depth_kernel, norm_gains, upstream):
    margin = KERNEL // 2
    frames = repack(loaded, plan)
    frame_rows = frames.reshape(-1, D).astype(jnp.float32)
    gain_pre = norm_gains[:, 0].astype(jnp.float32)
    gain_mid = norm_gains[:, 1].astype(jnp.float32)
    taps = depth_kernel.astype(jnp.float32)
    normed_full, pull_pre = jax.vjp(norm_rows, frame_rows, gain_pre)
    normed = normed_full.astype(jnp.bfloat16)
    hidden = jnp.dot(normed, in_weight, preferred_element_type=jnp.float32)
    gate_lin = hidden[:, :D]
    gate_sig = jax.nn.sigmoid(hidden[:, D:])
    gated = (gate_lin * gate_sig).astype(jnp.bfloat16).reshape(SLABS_ALL, SLAB, D)
    gated_pad = jnp.pad(gated, ((0, 0), (margin, margin), (0, 0)))
    id_pad = jnp.pad(segment_ids, ((0, 0), (margin, margin)), constant_values=-1)
    mixing = jnp.zeros((SLABS_ALL, SLAB, D), jnp.float32)
    for tap_index in range(KERNEL):
        same = (id_pad[:, tap_index:tap_index + SLAB] == segment_ids)[..., None]
        mixing = mixing + jnp.where(same, gated_pad[:, tap_index:tap_index + SLAB].astype(jnp.float32) * taps[:, tap_index], 0.0)
    activated_full, pull_mid = jax.vjp(mid_section, mixing.reshape(-1, D), gain_mid)
    activated = activated_full.astype(jnp.bfloat16)
    projected = jnp.dot(activated, out_weight, preferred_element_type=jnp.float32)
    encoded = (frame_rows + projected).astype(jnp.bfloat16).reshape(SLABS_ALL, SLAB, D)
    upstream_rows = upstream.reshape(-1, D)
    grad_act = jnp.dot(upstream_rows, out_weight.T, preferred_element_type=jnp.float32)
    grad_out_w = jnp.dot(activated.T, upstream_rows, preferred_element_type=jnp.float32)
    grad_mixing, grad_gain_mid = pull_mid(grad_act)
    grad_cells = grad_mixing.reshape(SLABS_ALL, SLAB, D)
    grad_pad = jnp.pad(grad_cells, ((0, 0), (margin, margin), (0, 0)))
    grad_gated = jnp.zeros((SLABS_ALL, SLAB, D), jnp.float32)
    tap_grads = []
    for tap_index in range(KERNEL):
        same = (id_pad[:, tap_index:tap_index + SLAB] == segment_ids)[..., None]
        tap_grads.append(lax.optimization_barrier(jnp.sum(jnp.where(same, grad_cells * gated_pad[:, tap_index:tap_index + SLAB].astype(jnp.float32), 0.0), axis=(0, 1))))
        mirror = 2 * margin - tap_index
        back_same = (id_pad[:, mirror:mirror + SLAB] == segment_ids)[..., None]
        grad_gated = grad_gated + jnp.where(back_same, grad_pad[:, mirror:mirror + SLAB] * taps[:, tap_index], 0.0)
    grad_taps = jnp.stack(tap_grads, axis=1)
    grad_gated = grad_gated.reshape(-1, D)
    grad_hidden = jnp.concatenate([grad_gated * gate_sig, grad_gated * gate_lin * gate_sig * (1.0 - gate_sig)], axis=1).astype(jnp.bfloat16)
    grad_in_w = jnp.dot(normed.T, grad_hidden, preferred_element_type=jnp.float32)
    grad_normed = jnp.dot(grad_hidden, in_weight.T, preferred_element_type=jnp.float32)
    grad_rows, grad_gain_pre = pull_pre(grad_normed)
    grad_frames = (upstream_rows.astype(jnp.float32) + grad_rows).astype(jnp.bfloat16).reshape(SLABS_ALL, SLAB, D)
    grad_gain = jnp.stack([grad_gain_pre, grad_gain_mid], axis=1)
    scale = 1.0 / math.sqrt(FRAMES_ALL)
    return (encoded, grad_frames, grad_in_w * scale, grad_out_w * scale, grad_taps * scale, grad_gain * scale)
```

```python
import functools
import math

import jax
import jax.numpy as jnp
from jax import lax
from jax.experimental import pallas as pl
from jax.experimental.pallas import tpu as pltpu
from jax.sharding import PartitionSpec as P

MESH = pl.DeviceIdType.MESH


def greet(p, q, n_dp, n_seq):
    barrier = pltpu.get_barrier_semaphore()

    @pl.loop(1, n_dp)
    def _(e):
        pl.semaphore_signal(
            barrier, inc=1, device_id=(lax.rem(p + e, n_dp), q), device_id_type=MESH
        )

    @pl.loop(1, n_seq)
    def _(d):
        pl.semaphore_signal(
            barrier, inc=1, device_id=(p, lax.rem(q + d, n_seq)), device_id_type=MESH
        )

    pl.semaphore_wait(barrier, n_dp + n_seq - 2)


def reduce_kernel(n_dp, n_seq, count, *refs):
    ins, outs, rest = refs[:count], refs[count : 2 * count], refs[2 * count :]
    own, peer, staged, inbox, final = (rest[i * count : (i + 1) * count] for i in range(5))
    load_sem, dp_send, dp_recv, rs_send, rs_recv, ag_send, ag_recv, keep_sem = rest[5 * count :]
    p, q = lax.axis_index("dp"), lax.axis_index("seq")
    greet(p, q, n_dp, n_seq)

    def to_dp(a, e, d):
        other = lax.rem(p + e, n_dp)
        return pltpu.make_async_remote_copy(
            src_ref=ins[a].at[other, lax.rem(q + d, n_seq)],
            dst_ref=peer[a].at[e - 1, d],
            send_sem=dp_send.at[a, e - 1, d],
            recv_sem=dp_recv.at[a, e - 1, d],
            device_id=(other, q),
            device_id_type=MESH,
        )

    def to_own(a, d):
        return pltpu.make_async_copy(
            ins[a].at[p, lax.rem(q + d, n_seq)], own[a].at[d], load_sem.at[a, d]
        )

    def to_seq(a, d):
        return pltpu.make_async_remote_copy(
            src_ref=staged[a].at[d],
            dst_ref=inbox[a].at[d],
            send_sem=rs_send.at[a, d],
            recv_sem=rs_recv.at[a, d],
            device_id=(p, lax.rem(q + d, n_seq)),
            device_id_type=MESH,
        )

    def to_all(a, d):
        return pltpu.make_async_remote_copy(
            src_ref=final[a],
            dst_ref=outs[a].at[q],
            send_sem=ag_send.at[a, d],
            recv_sem=ag_recv.at[a, d],
            device_id=(p, lax.rem(q + d, n_seq)),
            device_id_type=MESH,
        )

    @pl.loop(0, n_seq)
    def _(step):
        d = lax.rem(step + 1, n_seq)
        for a in range(count):
            to_own(a, d).start()

            @pl.loop(1, n_dp)
            def _(e):
                to_dp(a, e, d).start()

    def dp_sum(a, d):
        to_own(a, d).wait()
        total = own[a][d].astype(jnp.float32)
        for e in range(1, n_dp):
            to_dp(a, e, d).wait_recv()
            total = total + peer[a][e - 1, d].astype(jnp.float32)
        return total

    @pl.loop(1, n_seq)
    def _(d):
        for a in range(count):
            staged[a][d] = dp_sum(a, d).astype(staged[a].dtype)
            to_seq(a, d).start()

    for a in range(count):
        total = dp_sum(a, 0)

        def gather(d, value):
            to_seq(a, d).wait_recv()
            return value + inbox[a][d].astype(jnp.float32)

        total = lax.fori_loop(1, n_seq, gather, total)
        final[a][...] = total.astype(final[a].dtype)

        @pl.loop(1, n_seq)
        def _(d):
            to_all(a, d).start()

        pltpu.make_async_copy(final[a], outs[a].at[q], keep_sem.at[a]).start()

    @pl.loop(1, n_seq)
    def _(d):
        for a in range(count):
            to_seq(a, d).wait_send()
            to_all(a, d).wait_send()
            to_all(a, d).wait_recv()

    for a in range(count):
        pltpu.make_async_copy(final[a], outs[a].at[q], keep_sem.at[a]).wait()

        @pl.loop(0, n_seq)
        def _(d):
            @pl.loop(1, n_dp)
            def _(e):
                to_dp(a, e, d).wait_send()


def reduce_all(parts):
    n_dp, n_seq = lax.axis_size("dp"), lax.axis_size("seq")
    count = len(parts)
    dma = pltpu.SemaphoreType.DMA
    vmem = pltpu.VMEM
    tiles = [part.shape[2:] for part in parts]
    kinds = [part.dtype for part in parts]
    pairs = list(zip(tiles, kinds))
    return pl.pallas_call(
        functools.partial(reduce_kernel, n_dp, n_seq, count),
        out_shape=[jax.ShapeDtypeStruct((n_seq, *tile), kind) for tile, kind in pairs],
        in_specs=[pl.BlockSpec(memory_space=pl.ANY)] * count,
        out_specs=[pl.BlockSpec(memory_space=pl.ANY)] * count,
        scratch_shapes=(
            [vmem((n_seq, *tile), kind) for tile, kind in pairs]
            + [vmem((n_dp - 1, n_seq, *tile), kind) for tile, kind in pairs]
            + [vmem((n_seq, *tile), kind) for tile, kind in pairs]
            + [vmem((n_seq, *tile), kind) for tile, kind in pairs]
            + [vmem(tile, kind) for tile, kind in pairs]
            + [
                dma((count, n_seq)),
                dma((count, n_dp - 1, n_seq)),
                dma((count, n_dp - 1, n_seq)),
                dma((count, n_seq)),
                dma((count, n_seq)),
                dma((count, n_seq)),
                dma((count, n_seq)),
                dma((count,)),
            ]
        ),
        compiler_params=pltpu.CompilerParams(collective_id=0, has_side_effects=True),
        name="reduce_all",
    )(*parts)


def padded(block, sides, width):
    for axis, dim in sides:
        count = lax.axis_size(axis)
        forward = [(i, i + 1) for i in range(count - 1)]
        backward = [(target, source) for source, target in forward]
        low = lax.ppermute(
            lax.slice_in_dim(block, block.shape[dim] - width, None, axis=dim), axis, forward
        )
        high = lax.ppermute(lax.slice_in_dim(block, 0, width, axis=dim), axis, backward)
        block = jnp.concatenate([low, block, high], axis=dim)
    return block


def norm_rows(values, gain):
    average = jnp.mean(values, axis=-1, keepdims=True)
    centered = values - average
    spread = jnp.mean(centered * centered, axis=-1, keepdims=True)
    return centered * lax.rsqrt(spread + 1e-05) * gain


def mid_section(values, gain):
    normed = norm_rows(values, gain)
    return normed * jax.nn.sigmoid(normed)


def per_device(
    loaded, plan, segment_ids, in_weight, out_weight, depth_kernel, norm_gains, upstream
):
    rows_dev, width = loaded.shape
    devices = plan.shape[0]
    capacity = 2 * rows_dev // devices
    slabs, slab_len = segment_ids.shape
    frames_dev = slab_len // lax.axis_size("seq")
    kernel_len = depth_kernel.shape[1]
    margin = kernel_len // 2
    sender = lax.axis_index(("dp", "seq"))
    send_plan = lax.dynamic_index_in_dim(plan, sender, 0, keepdims=False)
    send_start = jnp.cumsum(send_plan) - send_plan
    slot_index = jnp.arange(capacity, dtype=jnp.int32)
    source_rows = send_start[:, None] + slot_index[None, :]
    filled = slot_index[None, :] < send_plan[:, None]
    picked = jnp.take(loaded, jnp.clip(source_rows, 0, rows_dev - 1).reshape(-1), axis=0)
    outgoing = jnp.where(filled.reshape(-1, 1), picked, jnp.zeros_like(picked)).reshape(
        devices, capacity, width
    )
    arrived = lax.all_to_all(
        outgoing, ("dp", "seq"), split_axis=0, concat_axis=0, tiled=True
    ).reshape(devices * capacity, width)
    recv_plan = lax.dynamic_index_in_dim(plan, sender, 1, keepdims=False)
    recv_end = jnp.cumsum(recv_plan)
    frame_index = jnp.arange(rows_dev, dtype=jnp.int32)
    before = recv_end[None, :] <= frame_index[:, None]
    source_dev = jnp.sum(before.astype(jnp.int32), axis=1)
    start_of = jnp.sum(jnp.where(before, recv_plan[None, :], 0), axis=1)
    frames = jnp.take(arrived, source_dev * capacity + frame_index - start_of, axis=0)
    kernel_full, gains_full = (
        lax.all_gather(depth_kernel, "dp", axis=0, tiled=True),
        lax.all_gather(norm_gains, "dp", axis=0, tiled=True),
    )
    taps = kernel_full.astype(jnp.float32)
    gain_pre = gains_full[:, 0].astype(jnp.float32)
    gain_mid = gains_full[:, 1].astype(jnp.float32)
    frame_rows = frames.astype(jnp.float32)
    normed_full, pull_pre = jax.vjp(norm_rows, frame_rows, gain_pre)
    normed = normed_full.astype(jnp.bfloat16)
    whole_in, whole_out = (
        lax.all_gather(in_weight, "dp", axis=0, tiled=True),
        lax.all_gather(out_weight, "dp", axis=0, tiled=True),
    )
    hidden = jnp.dot(normed, whole_in, preferred_element_type=jnp.float32)
    gate_lin = hidden[:, :width]
    gate_sig = jax.nn.sigmoid(hidden[:, width:])
    gated = (gate_lin * gate_sig).astype(jnp.bfloat16).reshape(slabs, frames_dev, width)
    gated_pad = padded(gated, (("seq", 1),), margin)
    id_pad = jnp.pad(segment_ids, ((0, 0), (margin, margin)), constant_values=-1)
    window = lax.dynamic_slice_in_dim(
        id_pad, lax.axis_index("seq") * frames_dev, frames_dev + 2 * margin, 1
    )
    center = window[:, margin : margin + frames_dev]
    mixing = jnp.zeros((slabs, frames_dev, width), jnp.float32)
    for tap_index in range(kernel_len):
        same = (window[:, tap_index : tap_index + frames_dev] == center)[..., None]
        mixing = mixing + jnp.where(
            same,
            gated_pad[:, tap_index : tap_index + frames_dev].astype(jnp.float32)
            * taps[:, tap_index],
            0.0,
        )
    activated_full, pull_mid = jax.vjp(mid_section, mixing.reshape(rows_dev, width), gain_mid)
    activated = activated_full.astype(jnp.bfloat16)
    upstream_rows = upstream.reshape(rows_dev, width)
    projected = jnp.dot(activated, whole_out, preferred_element_type=jnp.float32)
    grad_act = jnp.dot(upstream_rows, whole_out.T, preferred_element_type=jnp.float32)
    encoded = (frame_rows + projected).astype(jnp.bfloat16).reshape(slabs, frames_dev, width)
    grad_out_w = jnp.dot(activated.T, upstream_rows, preferred_element_type=jnp.float32)
    grad_mixing, grad_gain_mid = pull_mid(grad_act)
    grad_cells = grad_mixing.reshape(slabs, frames_dev, width)
    grad_pad = padded(grad_cells, (("seq", 1),), margin)
    grad_gated = jnp.zeros((slabs, frames_dev, width), jnp.float32)
    tap_grads = []
    for tap_index in range(kernel_len):
        same = (window[:, tap_index : tap_index + frames_dev] == center)[..., None]
        tap_grads.append(
            jnp.sum(
                jnp.where(
                    same,
                    grad_cells
                    * gated_pad[:, tap_index : tap_index + frames_dev].astype(jnp.float32),
                    0.0,
                ),
                axis=(0, 1),
            )
        )
        mirror = 2 * margin - tap_index
        back_same = (window[:, mirror : mirror + frames_dev] == center)[..., None]
        grad_gated = grad_gated + jnp.where(
            back_same, grad_pad[:, mirror : mirror + frames_dev] * taps[:, tap_index], 0.0
        )
    grad_taps = jnp.stack(tap_grads, axis=1)
    grad_gated = grad_gated.reshape(rows_dev, width)
    grad_hidden = jnp.concatenate(
        [grad_gated * gate_sig, grad_gated * gate_lin * gate_sig * (1.0 - gate_sig)], axis=1
    ).astype(jnp.bfloat16)
    grad_in_w = jnp.dot(normed.T, grad_hidden, preferred_element_type=jnp.float32)
    grad_normed = jnp.dot(grad_hidden, whole_in.T, preferred_element_type=jnp.float32)
    grad_rows, grad_gain_pre = pull_pre(grad_normed)
    grad_frames = (
        (upstream_rows.astype(jnp.float32) + grad_rows)
        .astype(jnp.bfloat16)
        .reshape(slabs, frames_dev, width)
    )
    n_dp, n_seq = lax.axis_size("dp"), lax.axis_size("seq")
    held = width // n_dp
    piece = held // n_seq
    smalls = jnp.concatenate([grad_taps.T, grad_gain_pre[None], grad_gain_mid[None]], axis=0)
    lines = smalls.shape[0]
    per_dev = lines * held // n_seq
    small_rows = -(-per_dev // 1024) * 8
    smalls = smalls.reshape(lines, n_dp, held).transpose(1, 0, 2).reshape(n_dp, n_seq, per_dev)
    smalls = jnp.pad(smalls, ((0, 0), (0, 0), (0, small_rows * 128 - per_dev)))
    sum_in, sum_out, sum_small = reduce_all(
        (
            grad_in_w.astype(jnp.bfloat16).reshape(n_dp, n_seq, piece, 2 * width),
            grad_out_w.astype(jnp.bfloat16).reshape(n_dp, n_seq, piece, width),
            smalls.reshape(n_dp, n_seq, small_rows, 128),
        )
    )
    scale = 1.0 / math.sqrt(n_dp * n_seq * rows_dev)
    small = sum_small.reshape(n_seq, -1)[:, :per_dev].reshape(lines, held).T * scale
    return (
        encoded,
        grad_frames,
        sum_in.reshape(held, 2 * width).astype(jnp.float32) * scale,
        sum_out.reshape(held, width).astype(jnp.float32) * scale,
        small[:, :kernel_len],
        small[:, kernel_len:],
    )


def solution(mesh):
    placed = (
        P(("dp", "seq"), None),
        P(),
        P("dp", None),
        P("dp", None),
        P("dp", None),
        P("dp", None),
        P("dp", None),
        P("dp", "seq", None),
    )
    return jax.shard_map(
        per_device,
        mesh=mesh,
        in_specs=placed,
        out_specs=(
            P("dp", "seq", None),
            P("dp", "seq", None),
            P("dp", None),
            P("dp", None),
            P("dp", None),
            P("dp", None),
        ),
        check_vma=False,
    )
```

```python
import functools
import math

import jax
import jax.numpy as jnp
from jax import lax
from jax.experimental import pallas as pl
from jax.experimental.pallas import tpu as pltpu
from jax.sharding import PartitionSpec as P

MESH = pl.DeviceIdType.MESH


FOLD = 2


def greet(partners):
    barrier = pltpu.get_barrier_semaphore()
    for partner in partners:
        pl.semaphore_signal(barrier, inc=1, device_id=partner, device_id_type=MESH)
    pl.semaphore_wait(barrier, len(partners))


def reduce_kernel(n_dp, n_seq, count, entries, *refs):
    far = n_seq // (FOLD * FOLD)
    ins, outs, rest = refs[:count], refs[count : 2 * count], refs[2 * count :]
    jobs = len(entries)
    own, peer, send1, in1, send2, in2, send3, in3, final = (
        rest[i * jobs : (i + 1) * jobs] for i in range(9)
    )
    sems = rest[9 * jobs :]
    p, q = lax.axis_index("dp"), lax.axis_index("seq")
    x, y, z = lax.rem(q, FOLD), lax.rem(q // FOLD, FOLD), q // (FOLD * FOLD)
    x_near = (p, q + 1 - 2 * x)
    y_near = (p, q + FOLD * (1 - 2 * y))
    plane = q - z * FOLD * FOLD
    z_far = [(p, lax.rem(z + 1 + i, far) * FOLD * FOLD + plane) for i in range(far - 1)]
    dp_far = [(lax.rem(p + 1 + e, n_dp), q) for e in range(n_dp - 1)]
    greet([*dp_far, x_near, y_near, *z_far])
    sent = []

    def remote(src, dst, send_sem, recv_sem, target):
        copy = pltpu.make_async_remote_copy(
            src_ref=src,
            dst_ref=dst,
            send_sem=send_sem,
            recv_sem=recv_sem,
            device_id=target,
            device_id_type=MESH,
        )
        copy.start()
        sent.append(copy)
        return copy

    def cols(j):
        return pl.ds(entries[j][1], entries[j][2])

    loads, dp_copies = {}, {}
    for i in range(far):
        zz = lax.rem(z + 1 + i, far)
        for j in range(jobs):
            a = entries[j][0]
            for e in range(n_dp - 1):
                dp_copies[i, j, e] = remote(
                    ins[a].at[dp_far[e][0], zz, :, :, :, cols(j)],
                    peer[j].at[e, i],
                    sems[0].at[j, e, i],
                    sems[1].at[j, e, i],
                    dp_far[e],
                )
            loads[i, j] = pltpu.make_async_copy(
                ins[a].at[p, zz, :, :, :, cols(j)], own[j].at[i], sems[2].at[j, i]
            )
            loads[i, j].start()

    def base(j, i, row, col):
        total = own[j][i, row, col].astype(jnp.float32)
        for e in range(n_dp - 1):
            total = total + peer[j][e, i, row, col].astype(jnp.float32)
        return total

    def at(j, first, second):
        return (second, first) if entries[j][3] else (first, second)

    steps1, steps2, steps3 = {}, {}, {}

    def stage1(j, i):
        loads[i, j].wait()
        for e in range(n_dp - 1):
            dp_copies[i, j, e].wait_recv()
        mine = x if entries[j][3] else y
        for other in range(FOLD):
            send1[j][i, other] = base(j, i, *at(j, 1 - mine, other)).astype(send1[j].dtype)
        steps1[i, j] = remote(
            send1[j].at[i],
            in1[j].at[i],
            sems[3].at[j, i],
            sems[4].at[j, i],
            x_near if entries[j][3] else y_near,
        )

    def stage2(j, i):
        steps1[i, j].wait_recv()
        mine, other = (x, 1 - y) if entries[j][3] else (y, 1 - x)
        total = base(j, i, *at(j, mine, other)) + in1[j][i, other].astype(jnp.float32)
        send2[j][i] = total.astype(send2[j].dtype)
        steps2[i, j] = remote(
            send2[j].at[i],
            in2[j].at[i],
            sems[5].at[j, i],
            sems[6].at[j, i],
            y_near if entries[j][3] else x_near,
        )

    def stage3(j, i):
        steps2[i, j].wait_recv()
        mine, other = (x, y) if entries[j][3] else (y, x)
        total = (
            base(j, i, *at(j, mine, other))
            + in1[j][i, other].astype(jnp.float32)
            + in2[j][i].astype(jnp.float32)
        )
        if i < far - 1:
            send3[j][i] = total.astype(send3[j].dtype)
            steps3[i, j] = remote(
                send3[j].at[i], in3[j].at[i], sems[7].at[j, i], sems[8].at[j, i], z_far[i]
            )
            return
        for i in range(far - 1):
            steps3[i, j].wait_recv()
            total = total + in3[j][i].astype(jnp.float32)
        final[j][...] = total.astype(final[j].dtype)

    for step in range(far + 1):
        for j in range(jobs):
            if step < far:
                stage1(j, step)
        for j in range(jobs):
            if 1 <= step < far + 1:
                stage2(j, step - 1)
        for j in range(jobs):
            if 2 <= step:
                stage3(j, step - 2)

    def place(j, zz, yy, xx):
        return outs[entries[j][0]].at[zz, yy, xx, :, cols(j)]

    keeps, hops_z, hops1, hops2 = [], {}, {}, {}

    def forward(j, i, src, zz):
        here = place(j, zz, y, x)
        hops1[i, j] = remote(
            src, here, sems[11].at[j, i], sems[12].at[j, i], y_near if entries[j][3] else x_near
        )
        hops2[i, j, 0] = remote(
            src,
            here,
            sems[13].at[j, 0, i],
            sems[14].at[j, 0, i],
            x_near if entries[j][3] else y_near,
        )

    for j in range(jobs):
        stage3(j, far - 1)
        here = place(j, z, y, x)
        for i in range(far - 1):
            hops_z[i, j] = remote(final[j], here, sems[9].at[j, i], sems[10].at[j, i], z_far[i])
        forward(j, far - 1, final[j], z)
        keep = pltpu.make_async_copy(final[j], here, sems[15].at[j])
        keep.start()
        keeps.append(keep)

    def relay(j, i, zz):
        hops1[i, j].wait_recv()
        there = place(j, zz, *((1 - y, x) if entries[j][3] else (y, 1 - x)))
        hops2[i, j, 1] = remote(
            there,
            there,
            sems[13].at[j, 1, i],
            sems[14].at[j, 1, i],
            x_near if entries[j][3] else y_near,
        )

    order = [far - 1, *range(far - 1)]
    for at_step, i in enumerate(order):
        if i < far - 1:
            zz = lax.rem(z + far - 1 - i, far)
            for j in range(jobs):
                hops_z[i, j].wait_recv()
                forward(j, i, place(j, zz, y, x), zz)
        if at_step:
            last = order[at_step - 1]
            for j in range(jobs):
                relay(j, last, lax.rem(z + 2 * far - 1 - last, far))
    for j in range(jobs):
        relay(j, order[-1], lax.rem(z + 2 * far - 1 - order[-1], far))
    for copy in hops2.values():
        copy.wait_recv()
    for keep in keeps:
        keep.wait()
    for copy in sent:
        copy.wait_send()


def reduce_all(parts):
    n_dp, n_seq = lax.axis_size("dp"), lax.axis_size("seq")
    far = n_seq // (FOLD * FOLD)
    count = len(parts)
    parts = [part.reshape(n_dp, far, FOLD, FOLD, *part.shape[2:]) for part in parts]
    entries = []
    for a, part in enumerate(parts):
        wide = part.shape[-1]
        if wide % 256:
            entries.append((a, 0, wide, True))
        else:
            entries.append((a, 0, wide // 2, True))
            entries.append((a, wide // 2, wide // 2, False))
    jobs = len(entries)
    dma = pltpu.SemaphoreType.DMA

    def slots(*lead):
        return [
            pltpu.VMEM((*lead, parts[a].shape[4], size), parts[a].dtype)
            for a, _, size, _ in entries
        ]

    results = pl.pallas_call(
        functools.partial(reduce_kernel, n_dp, n_seq, count, tuple(entries)),
        out_shape=[jax.ShapeDtypeStruct(part.shape[1:], part.dtype) for part in parts],
        in_specs=[pl.BlockSpec(memory_space=pl.ANY)] * count,
        out_specs=[pl.BlockSpec(memory_space=pl.ANY)] * count,
        scratch_shapes=(
            slots(far, FOLD, FOLD)
            + slots(n_dp - 1, far, FOLD, FOLD)
            + slots(far, FOLD)
            + slots(far, FOLD)
            + slots(far)
            + slots(far)
            + slots(far)
            + slots(far)
            + slots()
            + [dma((jobs, n_dp - 1, far))] * 2
            + [dma((jobs, far))] * 11
            + [dma((jobs, 2, far))] * 2
            + [dma((jobs,))]
        ),
        compiler_params=pltpu.CompilerParams(collective_id=0, has_side_effects=True),
        name="reduce_all",
    )(*parts)
    return [result.reshape(n_seq, *result.shape[3:]) for result in results]


def padded(block, sides, width):
    for axis, dim in sides:
        count = lax.axis_size(axis)
        forward = [(i, i + 1) for i in range(count - 1)]
        backward = [(target, source) for source, target in forward]
        low = lax.ppermute(
            lax.slice_in_dim(block, block.shape[dim] - width, None, axis=dim), axis, forward
        )
        high = lax.ppermute(lax.slice_in_dim(block, 0, width, axis=dim), axis, backward)
        block = jnp.concatenate([low, block, high], axis=dim)
    return block


def norm_rows(values, gain):
    average = jnp.mean(values, axis=-1, keepdims=True)
    centered = values - average
    spread = jnp.mean(centered * centered, axis=-1, keepdims=True)
    return centered * lax.rsqrt(spread + 1e-05) * gain


def mid_section(values, gain):
    normed = norm_rows(values, gain)
    return normed * jax.nn.sigmoid(normed)


def per_device(
    loaded, plan, segment_ids, in_weight, out_weight, depth_kernel, norm_gains, upstream
):
    rows_dev, width = loaded.shape
    devices = plan.shape[0]
    capacity = 2 * rows_dev // devices
    slabs, slab_len = segment_ids.shape
    frames_dev = slab_len // lax.axis_size("seq")
    kernel_len = depth_kernel.shape[1]
    margin = kernel_len // 2
    sender = lax.axis_index(("dp", "seq"))
    send_plan = lax.dynamic_index_in_dim(plan, sender, 0, keepdims=False)
    send_start = jnp.cumsum(send_plan) - send_plan
    slot_index = jnp.arange(capacity, dtype=jnp.int32)
    source_rows = send_start[:, None] + slot_index[None, :]
    filled = slot_index[None, :] < send_plan[:, None]
    picked = jnp.take(loaded, jnp.clip(source_rows, 0, rows_dev - 1).reshape(-1), axis=0)
    outgoing = jnp.where(filled.reshape(-1, 1), picked, jnp.zeros_like(picked)).reshape(
        devices, capacity, width
    )
    arrived = lax.all_to_all(
        outgoing, ("dp", "seq"), split_axis=0, concat_axis=0, tiled=True
    ).reshape(devices * capacity, width)
    recv_plan = lax.dynamic_index_in_dim(plan, sender, 1, keepdims=False)
    recv_end = jnp.cumsum(recv_plan)
    frame_index = jnp.arange(rows_dev, dtype=jnp.int32)
    before = recv_end[None, :] <= frame_index[:, None]
    source_dev = jnp.sum(before.astype(jnp.int32), axis=1)
    start_of = jnp.sum(jnp.where(before, recv_plan[None, :], 0), axis=1)
    frames = jnp.take(arrived, source_dev * capacity + frame_index - start_of, axis=0)
    kernel_full, gains_full = (
        lax.all_gather(depth_kernel, "dp", axis=0, tiled=True),
        lax.all_gather(norm_gains, "dp", axis=0, tiled=True),
    )
    taps = kernel_full.astype(jnp.float32)
    gain_pre = gains_full[:, 0].astype(jnp.float32)
    gain_mid = gains_full[:, 1].astype(jnp.float32)
    frame_rows = frames.astype(jnp.float32)
    normed_full, pull_pre = jax.vjp(norm_rows, frame_rows, gain_pre)
    normed = normed_full.astype(jnp.bfloat16)
    whole_in, whole_out = (
        lax.all_gather(in_weight, "dp", axis=0, tiled=True),
        lax.all_gather(out_weight, "dp", axis=0, tiled=True),
    )
    hidden = jnp.dot(normed, whole_in, preferred_element_type=jnp.float32)
    gate_lin = hidden[:, :width]
    gate_sig = jax.nn.sigmoid(hidden[:, width:])
    gated = (gate_lin * gate_sig).astype(jnp.bfloat16).reshape(slabs, frames_dev, width)
    gated_pad = padded(gated, (("seq", 1),), margin)
    id_pad = jnp.pad(segment_ids, ((0, 0), (margin, margin)), constant_values=-1)
    window = lax.dynamic_slice_in_dim(
        id_pad, lax.axis_index("seq") * frames_dev, frames_dev + 2 * margin, 1
    )
    center = window[:, margin : margin + frames_dev]
    mixing = jnp.zeros((slabs, frames_dev, width), jnp.float32)
    for tap_index in range(kernel_len):
        same = (window[:, tap_index : tap_index + frames_dev] == center)[..., None]
        mixing = mixing + jnp.where(
            same,
            gated_pad[:, tap_index : tap_index + frames_dev].astype(jnp.float32)
            * taps[:, tap_index],
            0.0,
        )
    activated_full, pull_mid = jax.vjp(mid_section, mixing.reshape(rows_dev, width), gain_mid)
    activated = activated_full.astype(jnp.bfloat16)
    upstream_rows = upstream.reshape(rows_dev, width)
    projected = jnp.dot(activated, whole_out, preferred_element_type=jnp.float32)
    grad_act = jnp.dot(upstream_rows, whole_out.T, preferred_element_type=jnp.float32)
    encoded = (frame_rows + projected).astype(jnp.bfloat16).reshape(slabs, frames_dev, width)
    grad_out_w = jnp.dot(activated.T, upstream_rows, preferred_element_type=jnp.float32)
    grad_mixing, grad_gain_mid = pull_mid(grad_act)
    grad_cells = grad_mixing.reshape(slabs, frames_dev, width)
    grad_pad = padded(grad_cells, (("seq", 1),), margin)
    grad_gated = jnp.zeros((slabs, frames_dev, width), jnp.float32)
    tap_grads = []
    for tap_index in range(kernel_len):
        same = (window[:, tap_index : tap_index + frames_dev] == center)[..., None]
        tap_grads.append(
            jnp.sum(
                jnp.where(
                    same,
                    grad_cells
                    * gated_pad[:, tap_index : tap_index + frames_dev].astype(jnp.float32),
                    0.0,
                ),
                axis=(0, 1),
            )
        )
        mirror = 2 * margin - tap_index
        back_same = (window[:, mirror : mirror + frames_dev] == center)[..., None]
        grad_gated = grad_gated + jnp.where(
            back_same, grad_pad[:, mirror : mirror + frames_dev] * taps[:, tap_index], 0.0
        )
    grad_taps = jnp.stack(tap_grads, axis=1)
    grad_gated = grad_gated.reshape(rows_dev, width)
    grad_hidden = jnp.concatenate(
        [grad_gated * gate_sig, grad_gated * gate_lin * gate_sig * (1.0 - gate_sig)], axis=1
    ).astype(jnp.bfloat16)
    grad_in_w = jnp.dot(normed.T, grad_hidden, preferred_element_type=jnp.float32)
    grad_normed = jnp.dot(grad_hidden, whole_in.T, preferred_element_type=jnp.float32)
    grad_rows, grad_gain_pre = pull_pre(grad_normed)
    grad_frames = (
        (upstream_rows.astype(jnp.float32) + grad_rows)
        .astype(jnp.bfloat16)
        .reshape(slabs, frames_dev, width)
    )
    n_dp, n_seq = lax.axis_size("dp"), lax.axis_size("seq")
    held = width // n_dp
    piece = held // n_seq
    smalls = jnp.concatenate([grad_taps.T, grad_gain_pre[None], grad_gain_mid[None]], axis=0)
    lines = smalls.shape[0]
    per_dev = lines * held // n_seq
    small_rows = -(-per_dev // 1024) * 8
    smalls = smalls.reshape(lines, n_dp, held).transpose(1, 0, 2).reshape(n_dp, n_seq, per_dev)
    smalls = jnp.pad(smalls, ((0, 0), (0, 0), (0, small_rows * 128 - per_dev)))
    sum_in, sum_out, sum_small = reduce_all(
        (
            grad_in_w.astype(jnp.bfloat16).reshape(n_dp, n_seq, piece, 2 * width),
            grad_out_w.astype(jnp.bfloat16).reshape(n_dp, n_seq, piece, width),
            smalls.reshape(n_dp, n_seq, small_rows, 128),
        )
    )
    scale = 1.0 / math.sqrt(n_dp * n_seq * rows_dev)
    small = sum_small.reshape(n_seq, -1)[:, :per_dev].reshape(lines, held).T * scale
    return (
        encoded,
        grad_frames,
        sum_in.reshape(held, 2 * width).astype(jnp.float32) * scale,
        sum_out.reshape(held, width).astype(jnp.float32) * scale,
        small[:, :kernel_len],
        small[:, kernel_len:],
    )


def solution(mesh):
    placed = (
        P(("dp", "seq"), None),
        P(),
        P("dp", None),
        P("dp", None),
        P("dp", None),
        P("dp", None),
        P("dp", None),
        P("dp", "seq", None),
    )
    return jax.shard_map(
        per_device,
        mesh=mesh,
        in_specs=placed,
        out_specs=(
            P("dp", "seq", None),
            P("dp", "seq", None),
            P("dp", None),
            P("dp", None),
            P("dp", None),
            P("dp", None),
        ),
        check_vma=False,
    )
```

```python
import functools
import math

import jax
import jax.numpy as jnp
from jax import lax
from jax.experimental import pallas as pl
from jax.experimental.pallas import tpu as pltpu
from jax.sharding import PartitionSpec as P

MESH = pl.DeviceIdType.MESH


FOLD = 2


def greet(partners):
    barrier = pltpu.get_barrier_semaphore()
    for partner in partners:
        pl.semaphore_signal(barrier, inc=1, device_id=partner, device_id_type=MESH)
    pl.semaphore_wait(barrier, len(partners))


def reduce_kernel(n_dp, n_seq, count, entries, *refs):
    far = n_seq // (FOLD * FOLD)
    ins, outs, rest = refs[:count], refs[count : 2 * count], refs[2 * count :]
    jobs = len(entries)
    own, peer, send1, in1, send2, in2, send3, in3, final = (
        rest[i * jobs : (i + 1) * jobs] for i in range(9)
    )
    sems = rest[9 * jobs :]
    p, q = lax.axis_index("dp"), lax.axis_index("seq")
    x, y, z = lax.rem(q, FOLD), lax.rem(q // FOLD, FOLD), q // (FOLD * FOLD)
    x_near = (p, q + 1 - 2 * x)
    y_near = (p, q + FOLD * (1 - 2 * y))
    plane = q - z * FOLD * FOLD
    z_far = [(p, lax.rem(z + 1 + i, far) * FOLD * FOLD + plane) for i in range(far - 1)]
    dp_far = [(lax.rem(p + 1 + e, n_dp), q) for e in range(n_dp - 1)]
    greet([*dp_far, x_near, y_near, *z_far])
    sent = []

    def remote(src, dst, send_sem, recv_sem, target):
        copy = pltpu.make_async_remote_copy(
            src_ref=src,
            dst_ref=dst,
            send_sem=send_sem,
            recv_sem=recv_sem,
            device_id=target,
            device_id_type=MESH,
        )
        copy.start()
        sent.append(copy)
        return copy

    def cols(j):
        return pl.ds(entries[j][1], entries[j][2])

    loads, dp_copies = {}, {}
    for i in range(far):
        zz = lax.rem(z + 1 + i, far)
        for j in range(jobs):
            a = entries[j][0]
            for e in range(n_dp - 1):
                dp_copies[i, j, e] = remote(
                    ins[a].at[dp_far[e][0], zz, :, :, :, cols(j)],
                    peer[j].at[e, i],
                    sems[0].at[j, e, i],
                    sems[1].at[j, e, i],
                    dp_far[e],
                )
            loads[i, j] = pltpu.make_async_copy(
                ins[a].at[p, zz, :, :, :, cols(j)], own[j].at[i], sems[2].at[j, i]
            )
            loads[i, j].start()

    def base(j, i, row, col):
        total = own[j][i, row, col].astype(jnp.float32)
        for e in range(n_dp - 1):
            total = total + peer[j][e, i, row, col].astype(jnp.float32)
        return total

    def at(j, first, second):
        return (second, first) if entries[j][3] else (first, second)

    steps1, steps2, steps3 = {}, {}, {}

    def stage1(j, i):
        loads[i, j].wait()
        for e in range(n_dp - 1):
            dp_copies[i, j, e].wait_recv()
        mine = x if entries[j][3] else y
        for other in range(FOLD):
            send1[j][i, other] = base(j, i, *at(j, 1 - mine, other)).astype(send1[j].dtype)
        steps1[i, j] = remote(
            send1[j].at[i],
            in1[j].at[i],
            sems[3].at[j, i],
            sems[4].at[j, i],
            x_near if entries[j][3] else y_near,
        )

    def stage2(j, i):
        steps1[i, j].wait_recv()
        mine, other = (x, 1 - y) if entries[j][3] else (y, 1 - x)
        total = base(j, i, *at(j, mine, other)) + in1[j][i, other].astype(jnp.float32)
        send2[j][i] = total.astype(send2[j].dtype)
        steps2[i, j] = remote(
            send2[j].at[i],
            in2[j].at[i],
            sems[5].at[j, i],
            sems[6].at[j, i],
            y_near if entries[j][3] else x_near,
        )

    def stage3(j, i):
        steps2[i, j].wait_recv()
        mine, other = (x, y) if entries[j][3] else (y, x)
        total = (
            base(j, i, *at(j, mine, other))
            + in1[j][i, other].astype(jnp.float32)
            + in2[j][i].astype(jnp.float32)
        )
        if i < far - 1:
            send3[j][i] = total.astype(send3[j].dtype)
            steps3[i, j] = remote(
                send3[j].at[i], in3[j].at[i], sems[7].at[j, i], sems[8].at[j, i], z_far[i]
            )
            return
        for i in range(far - 1):
            steps3[i, j].wait_recv()
            total = total + in3[j][i].astype(jnp.float32)
        final[j][...] = total.astype(final[j].dtype)

    for step in range(far + 1):
        for j in range(jobs):
            if step < far:
                stage1(j, step)
        for j in range(jobs):
            if 1 <= step < far + 1:
                stage2(j, step - 1)
        for j in range(jobs):
            if 2 <= step:
                stage3(j, step - 2)

    def place(j, zz, yy, xx):
        return outs[entries[j][0]].at[zz, yy, xx, :, cols(j)]

    keeps, hops_z, hops1, hops2 = [], {}, {}, {}

    def forward(j, i, src, zz):
        here = place(j, zz, y, x)
        hops1[i, j] = remote(
            src, here, sems[11].at[j, i], sems[12].at[j, i], y_near if entries[j][3] else x_near
        )
        hops2[i, j, 0] = remote(
            src,
            here,
            sems[13].at[j, 0, i],
            sems[14].at[j, 0, i],
            x_near if entries[j][3] else y_near,
        )

    for j in range(jobs):
        stage3(j, far - 1)
        here = place(j, z, y, x)
        for i in range(far - 1):
            hops_z[i, j] = remote(final[j], here, sems[9].at[j, i], sems[10].at[j, i], z_far[i])
        forward(j, far - 1, final[j], z)
        keep = pltpu.make_async_copy(final[j], here, sems[15].at[j])
        keep.start()
        keeps.append(keep)

    def relay(j, i, zz):
        hops1[i, j].wait_recv()
        there = place(j, zz, *((1 - y, x) if entries[j][3] else (y, 1 - x)))
        hops2[i, j, 1] = remote(
            there,
            there,
            sems[13].at[j, 1, i],
            sems[14].at[j, 1, i],
            x_near if entries[j][3] else y_near,
        )

    order = [far - 1, *range(far - 1)]
    for at_step, i in enumerate(order):
        if i < far - 1:
            zz = lax.rem(z + far - 1 - i, far)
            for j in range(jobs):
                hops_z[i, j].wait_recv()
                forward(j, i, place(j, zz, y, x), zz)
        if at_step:
            last = order[at_step - 1]
            for j in range(jobs):
                relay(j, last, lax.rem(z + 2 * far - 1 - last, far))
    for j in range(jobs):
        relay(j, order[-1], lax.rem(z + 2 * far - 1 - order[-1], far))
    for copy in hops2.values():
        copy.wait_recv()
    for keep in keeps:
        keep.wait()
    for copy in sent:
        copy.wait_send()


def reduce_all(parts):
    n_dp, n_seq = lax.axis_size("dp"), lax.axis_size("seq")
    far = n_seq // (FOLD * FOLD)
    count = len(parts)
    parts = [part.reshape(n_dp, far, FOLD, FOLD, *part.shape[2:]) for part in parts]
    entries = []
    for a, part in enumerate(parts):
        wide = part.shape[-1]
        if wide % 256:
            entries.append((a, 0, wide, True))
        else:
            entries.append((a, 0, wide // 2, True))
            entries.append((a, wide // 2, wide // 2, False))
    jobs = len(entries)
    dma = pltpu.SemaphoreType.DMA

    def slots(*lead):
        return [
            pltpu.VMEM((*lead, parts[a].shape[4], size), parts[a].dtype)
            for a, _, size, _ in entries
        ]

    results = pl.pallas_call(
        functools.partial(reduce_kernel, n_dp, n_seq, count, tuple(entries)),
        out_shape=[jax.ShapeDtypeStruct(part.shape[1:], part.dtype) for part in parts],
        in_specs=[pl.BlockSpec(memory_space=pl.ANY)] * count,
        out_specs=[pl.BlockSpec(memory_space=pl.ANY)] * count,
        scratch_shapes=(
            slots(far, FOLD, FOLD)
            + slots(n_dp - 1, far, FOLD, FOLD)
            + slots(far, FOLD)
            + slots(far, FOLD)
            + slots(far)
            + slots(far)
            + slots(far)
            + slots(far)
            + slots()
            + [dma((jobs, n_dp - 1, far))] * 2
            + [dma((jobs, far))] * 11
            + [dma((jobs, 2, far))] * 2
            + [dma((jobs,))]
        ),
        compiler_params=pltpu.CompilerParams(collective_id=0, has_side_effects=True),
        name="reduce_all",
    )(*parts)
    return [result.reshape(n_seq, *result.shape[3:]) for result in results]


TILE = 16
LANES = 128


def spread(source, target, frames, taps):
    for shift in range(min(8, taps)):
        rows = frames + 8 * ((taps - 1 - shift) // 8)
        for s in range(source.shape[0]):
            target[shift, s, :rows, :] = source[s, shift : shift + rows, :]


def tap_rows(ref, s, row, k, lanes):
    start = pl.multiple_of(row + 8 * (k // 8), 8)
    return ref[k % 8, s, pl.ds(start, TILE), lanes]


def mix_kernel(id_ref, gated_ref, tap_ref, out_ref, ids, gated):
    slabs, frames, width = out_ref.shape
    taps = tap_ref.shape[0]
    spread(id_ref, ids, frames, taps)
    spread(gated_ref, gated, frames, taps)
    every = pl.ds(0, LANES)

    @pl.loop(0, slabs)
    def _(s):
        @pl.loop(0, frames // TILE)
        def _(tile):
            row = pl.multiple_of(tile * TILE, TILE)
            center = tap_rows(ids, s, row, taps // 2, every)
            totals = [jnp.zeros((TILE, LANES), jnp.float32) for _ in range(width // LANES)]
            for k in range(taps):
                same = tap_rows(ids, s, row, k, every) == center
                for c in range(width // LANES):
                    lanes = pl.ds(c * LANES, LANES)
                    term = tap_rows(gated, s, row, k, lanes) * tap_ref[k : k + 1, lanes]
                    totals[c] = totals[c] + jnp.where(same, term, 0.0)
            for c in range(width // LANES):
                out_ref[s, pl.ds(row, TILE), pl.ds(c * LANES, LANES)] = totals[c]


def unmix_kernel(
    id_ref, gated_ref, grad_ref, tap_ref, out_ref, tap_out_ref, sums, ids, gated, grad
):
    slabs, frames, width = out_ref.shape
    taps = tap_ref.shape[0]
    margin = taps // 2
    spread(id_ref, ids, frames, taps)
    spread(gated_ref, gated, frames, taps)
    spread(grad_ref, grad, frames, taps)
    sums[...] = jnp.zeros_like(sums)
    every = pl.ds(0, LANES)

    @pl.loop(0, slabs)
    def _(s):
        @pl.loop(0, frames // TILE)
        def _(tile):
            row = pl.multiple_of(tile * TILE, TILE)
            center = tap_rows(ids, s, row, margin, every)
            totals = [jnp.zeros((TILE, LANES), jnp.float32) for _ in range(width // LANES)]
            for k in range(taps):
                same = tap_rows(ids, s, row, k, every) == center
                mirror = taps - 1 - k
                for c in range(width // LANES):
                    lanes = pl.ds(c * LANES, LANES)
                    term = tap_rows(grad, s, row, k, lanes) * tap_ref[mirror : mirror + 1, lanes]
                    totals[c] = totals[c] + jnp.where(same, term, 0.0)
                    here = tap_rows(grad, s, row, margin, lanes)
                    cross = jnp.where(same, here * tap_rows(gated, s, row, k, lanes), 0.0)
                    folded = cross[:8]
                    for piece in range(8, TILE, 8):
                        folded = folded + cross[piece : piece + 8]
                    sums[k, :, lanes] = sums[k, :, lanes] + folded
            for c in range(width // LANES):
                out_ref[s, pl.ds(row, TILE), pl.ds(c * LANES, LANES)] = totals[c]

    for k in range(taps):
        tap_out_ref[k : k + 1, :] = jnp.sum(sums[k], axis=0, keepdims=True)


def local_call(kernel, out_shape, scratch, *args):
    whole = pl.BlockSpec(memory_space=pltpu.VMEM)
    return pl.pallas_call(
        kernel,
        out_shape=out_shape,
        in_specs=[whole] * len(args),
        out_specs=jax.tree.map(lambda _: whole, out_shape),
        scratch_shapes=scratch,
    )(*args)


def padded(block, sides, width):
    for axis, dim in sides:
        count = lax.axis_size(axis)
        forward = [(i, i + 1) for i in range(count - 1)]
        backward = [(target, source) for source, target in forward]
        low = lax.ppermute(
            lax.slice_in_dim(block, block.shape[dim] - width, None, axis=dim), axis, forward
        )
        high = lax.ppermute(lax.slice_in_dim(block, 0, width, axis=dim), axis, backward)
        block = jnp.concatenate([low, block, high], axis=dim)
    return block


def norm_rows(values, gain):
    average = jnp.mean(values, axis=-1, keepdims=True)
    centered = values - average
    spread = jnp.mean(centered * centered, axis=-1, keepdims=True)
    return centered * lax.rsqrt(spread + 1e-05) * gain


def mid_section(values, gain):
    normed = norm_rows(values, gain)
    return normed * jax.nn.sigmoid(normed)


def per_device(
    loaded, plan, segment_ids, in_weight, out_weight, depth_kernel, norm_gains, upstream
):
    rows_dev, width = loaded.shape
    devices = plan.shape[0]
    capacity = 2 * rows_dev // devices
    slabs, slab_len = segment_ids.shape
    frames_dev = slab_len // lax.axis_size("seq")
    kernel_len = depth_kernel.shape[1]
    margin = kernel_len // 2
    sender = lax.axis_index(("dp", "seq"))
    send_plan = lax.dynamic_index_in_dim(plan, sender, 0, keepdims=False)
    send_start = jnp.cumsum(send_plan) - send_plan
    slot_index = jnp.arange(capacity, dtype=jnp.int32)
    source_rows = send_start[:, None] + slot_index[None, :]
    filled = slot_index[None, :] < send_plan[:, None]
    picked = jnp.take(loaded, jnp.clip(source_rows, 0, rows_dev - 1).reshape(-1), axis=0)
    outgoing = jnp.where(filled.reshape(-1, 1), picked, jnp.zeros_like(picked)).reshape(
        devices, capacity, width
    )
    arrived = lax.all_to_all(
        outgoing, ("dp", "seq"), split_axis=0, concat_axis=0, tiled=True
    ).reshape(devices * capacity, width)
    recv_plan = lax.dynamic_index_in_dim(plan, sender, 1, keepdims=False)
    recv_end = jnp.cumsum(recv_plan)
    frame_index = jnp.arange(rows_dev, dtype=jnp.int32)
    before = recv_end[None, :] <= frame_index[:, None]
    source_dev = jnp.sum(before.astype(jnp.int32), axis=1)
    start_of = jnp.sum(jnp.where(before, recv_plan[None, :], 0), axis=1)
    frames = jnp.take(arrived, source_dev * capacity + frame_index - start_of, axis=0)
    kernel_full, gains_full = (
        lax.all_gather(depth_kernel, "dp", axis=0, tiled=True),
        lax.all_gather(norm_gains, "dp", axis=0, tiled=True),
    )
    taps = kernel_full.astype(jnp.float32)
    gain_pre = gains_full[:, 0].astype(jnp.float32)
    gain_mid = gains_full[:, 1].astype(jnp.float32)
    frame_rows = frames.astype(jnp.float32)
    normed_full, pull_pre = jax.vjp(norm_rows, frame_rows, gain_pre)
    normed = normed_full.astype(jnp.bfloat16)
    whole_in, whole_out = (
        lax.all_gather(in_weight, "dp", axis=0, tiled=True),
        lax.all_gather(out_weight, "dp", axis=0, tiled=True),
    )
    hidden = jnp.dot(normed, whole_in, preferred_element_type=jnp.float32)
    gate_lin = hidden[:, :width]
    gate_sig = jax.nn.sigmoid(hidden[:, width:])
    gated = (gate_lin * gate_sig).astype(jnp.bfloat16).reshape(slabs, frames_dev, width)
    gated_pad = padded(gated, (("seq", 1),), margin)
    id_pad = jnp.pad(segment_ids, ((0, 0), (margin, margin)), constant_values=-1)
    window = lax.dynamic_slice_in_dim(
        id_pad, lax.axis_index("seq") * frames_dev, frames_dev + 2 * margin, 1
    )
    ids = jnp.broadcast_to(window[:, :, None], (*window.shape, LANES))
    gated_rows = gated_pad.astype(jnp.float32)
    taps = taps.T
    reach = frames_dev + 8 * ((kernel_len - 1) // 8)
    spread_ids = pltpu.VMEM((8, slabs, reach, LANES), jnp.int32)
    spread_rows = pltpu.VMEM((8, slabs, reach, width), jnp.float32)
    mixing = local_call(
        mix_kernel,
        jax.ShapeDtypeStruct((slabs, frames_dev, width), jnp.float32),
        [spread_ids, spread_rows],
        ids,
        gated_rows,
        taps,
    )
    activated_full, pull_mid = jax.vjp(mid_section, mixing.reshape(rows_dev, width), gain_mid)
    activated = activated_full.astype(jnp.bfloat16)
    upstream_rows = upstream.reshape(rows_dev, width)
    projected = jnp.dot(activated, whole_out, preferred_element_type=jnp.float32)
    grad_act = jnp.dot(upstream_rows, whole_out.T, preferred_element_type=jnp.float32)
    encoded = (frame_rows + projected).astype(jnp.bfloat16).reshape(slabs, frames_dev, width)
    grad_out_w = jnp.dot(activated.T, upstream_rows, preferred_element_type=jnp.float32)
    grad_mixing, grad_gain_mid = pull_mid(grad_act)
    grad_cells = grad_mixing.reshape(slabs, frames_dev, width)
    grad_pad = padded(grad_cells, (("seq", 1),), margin)
    grad_gated, grad_taps = local_call(
        unmix_kernel,
        (
            jax.ShapeDtypeStruct((slabs, frames_dev, width), jnp.float32),
            jax.ShapeDtypeStruct((kernel_len, width), jnp.float32),
        ),
        [
            pltpu.VMEM((kernel_len, 8, width), jnp.float32),
            spread_ids,
            spread_rows,
            spread_rows,
        ],
        ids,
        gated_rows,
        grad_pad,
        taps,
    )
    grad_gated = grad_gated.reshape(rows_dev, width)
    grad_hidden = jnp.concatenate(
        [grad_gated * gate_sig, grad_gated * gate_lin * gate_sig * (1.0 - gate_sig)], axis=1
    ).astype(jnp.bfloat16)
    grad_in_w = jnp.dot(normed.T, grad_hidden, preferred_element_type=jnp.float32)
    grad_normed = jnp.dot(grad_hidden, whole_in.T, preferred_element_type=jnp.float32)
    grad_rows, grad_gain_pre = pull_pre(grad_normed)
    grad_frames = (
        (upstream_rows.astype(jnp.float32) + grad_rows)
        .astype(jnp.bfloat16)
        .reshape(slabs, frames_dev, width)
    )
    n_dp, n_seq = lax.axis_size("dp"), lax.axis_size("seq")
    held = width // n_dp
    piece = held // n_seq
    smalls = jnp.concatenate([grad_taps, grad_gain_pre[None], grad_gain_mid[None]], axis=0)
    lines = smalls.shape[0]
    per_dev = lines * held // n_seq
    small_rows = -(-per_dev // 1024) * 8
    smalls = smalls.reshape(lines, n_dp, held).transpose(1, 0, 2).reshape(n_dp, n_seq, per_dev)
    smalls = jnp.pad(smalls, ((0, 0), (0, 0), (0, small_rows * 128 - per_dev)))
    sum_in, sum_out, sum_small = reduce_all(
        (
            grad_in_w.astype(jnp.bfloat16).reshape(n_dp, n_seq, piece, 2 * width),
            grad_out_w.astype(jnp.bfloat16).reshape(n_dp, n_seq, piece, width),
            smalls.reshape(n_dp, n_seq, small_rows, 128),
        )
    )
    scale = 1.0 / math.sqrt(n_dp * n_seq * rows_dev)
    small = sum_small.reshape(n_seq, -1)[:, :per_dev].reshape(lines, held).T * scale
    return (
        encoded,
        grad_frames,
        sum_in.reshape(held, 2 * width).astype(jnp.float32) * scale,
        sum_out.reshape(held, width).astype(jnp.float32) * scale,
        small[:, :kernel_len],
        small[:, kernel_len:],
    )


def solution(mesh):
    placed = (
        P(("dp", "seq"), None),
        P(),
        P("dp", None),
        P("dp", None),
        P("dp", None),
        P("dp", None),
        P("dp", None),
        P("dp", "seq", None),
    )
    return jax.shard_map(
        per_device,
        mesh=mesh,
        in_specs=placed,
        out_specs=(
            P("dp", "seq", None),
            P("dp", "seq", None),
            P("dp", None),
            P("dp", None),
            P("dp", None),
            P("dp", None),
        ),
        check_vma=False,
    )
```

```python
import functools
import math

import jax
import jax.numpy as jnp
from jax import lax
from jax.experimental import pallas as pl
from jax.experimental.pallas import tpu as pltpu
from jax.sharding import PartitionSpec as P

MESH = pl.DeviceIdType.MESH


FOLD = 2


def greet(partners):
    barrier = pltpu.get_barrier_semaphore()
    for partner in partners:
        pl.semaphore_signal(barrier, inc=1, device_id=partner, device_id_type=MESH)
    pl.semaphore_wait(barrier, len(partners))


def reduce_kernel(n_dp, n_seq, count, entries, *refs):
    far = n_seq // (FOLD * FOLD)
    ins, outs, rest = refs[:count], refs[count : 2 * count], refs[2 * count :]
    jobs = len(entries)
    own, peer, send1, in1, send2, in2, send3, in3, final = (
        rest[i * jobs : (i + 1) * jobs] for i in range(9)
    )
    sems = rest[9 * jobs :]
    p, q = lax.axis_index("dp"), lax.axis_index("seq")
    x, y, z = lax.rem(q, FOLD), lax.rem(q // FOLD, FOLD), q // (FOLD * FOLD)
    x_near = (p, q + 1 - 2 * x)
    y_near = (p, q + FOLD * (1 - 2 * y))
    plane = q - z * FOLD * FOLD
    z_far = [(p, lax.rem(z + 1 + i, far) * FOLD * FOLD + plane) for i in range(far - 1)]
    dp_far = [(lax.rem(p + 1 + e, n_dp), q) for e in range(n_dp - 1)]
    greet([*dp_far, x_near, y_near, *z_far])
    sent = []

    def remote(src, dst, send_sem, recv_sem, target):
        copy = pltpu.make_async_remote_copy(
            src_ref=src,
            dst_ref=dst,
            send_sem=send_sem,
            recv_sem=recv_sem,
            device_id=target,
            device_id_type=MESH,
        )
        copy.start()
        sent.append(copy)
        return copy

    def cols(j):
        return pl.ds(entries[j][1], entries[j][2])

    loads, dp_copies = {}, {}
    for i in range(far):
        zz = lax.rem(z + 1 + i, far)
        for j in range(jobs):
            a = entries[j][0]
            for e in range(n_dp - 1):
                dp_copies[i, j, e] = remote(
                    ins[a].at[dp_far[e][0], zz, :, :, :, cols(j)],
                    peer[j].at[e, i],
                    sems[0].at[j, e, i],
                    sems[1].at[j, e, i],
                    dp_far[e],
                )
            loads[i, j] = pltpu.make_async_copy(
                ins[a].at[p, zz, :, :, :, cols(j)], own[j].at[i], sems[2].at[j, i]
            )
            loads[i, j].start()

    def base(j, i, row, col):
        total = own[j][i, row, col].astype(jnp.float32)
        for e in range(n_dp - 1):
            total = total + peer[j][e, i, row, col].astype(jnp.float32)
        return total

    def at(j, first, second):
        return (second, first) if entries[j][3] else (first, second)

    steps1, steps2, steps3 = {}, {}, {}

    def stage1(j, i):
        loads[i, j].wait()
        for e in range(n_dp - 1):
            dp_copies[i, j, e].wait_recv()
        mine = x if entries[j][3] else y
        for other in range(FOLD):
            send1[j][i, other] = base(j, i, *at(j, 1 - mine, other)).astype(send1[j].dtype)
        steps1[i, j] = remote(
            send1[j].at[i],
            in1[j].at[i],
            sems[3].at[j, i],
            sems[4].at[j, i],
            x_near if entries[j][3] else y_near,
        )

    def stage2(j, i):
        steps1[i, j].wait_recv()
        mine, other = (x, 1 - y) if entries[j][3] else (y, 1 - x)
        total = base(j, i, *at(j, mine, other)) + in1[j][i, other].astype(jnp.float32)
        send2[j][i] = total.astype(send2[j].dtype)
        steps2[i, j] = remote(
            send2[j].at[i],
            in2[j].at[i],
            sems[5].at[j, i],
            sems[6].at[j, i],
            y_near if entries[j][3] else x_near,
        )

    def stage3(j, i):
        steps2[i, j].wait_recv()
        mine, other = (x, y) if entries[j][3] else (y, x)
        total = (
            base(j, i, *at(j, mine, other))
            + in1[j][i, other].astype(jnp.float32)
            + in2[j][i].astype(jnp.float32)
        )
        if i < far - 1:
            send3[j][i] = total.astype(send3[j].dtype)
            steps3[i, j] = remote(
                send3[j].at[i], in3[j].at[i], sems[7].at[j, i], sems[8].at[j, i], z_far[i]
            )
            return
        for i in range(far - 1):
            steps3[i, j].wait_recv()
            total = total + in3[j][i].astype(jnp.float32)
        final[j][...] = total.astype(final[j].dtype)

    for step in range(far + 1):
        for j in range(jobs):
            if step < far:
                stage1(j, step)
        for j in range(jobs):
            if 1 <= step < far + 1:
                stage2(j, step - 1)
        for j in range(jobs):
            if 2 <= step:
                stage3(j, step - 2)

    def place(j, zz, yy, xx):
        return outs[entries[j][0]].at[zz, yy, xx, :, cols(j)]

    keeps, hops_z, hops1, hops2 = [], {}, {}, {}

    def forward(j, i, src, zz):
        here = place(j, zz, y, x)
        hops1[i, j] = remote(
            src, here, sems[11].at[j, i], sems[12].at[j, i], y_near if entries[j][3] else x_near
        )
        hops2[i, j, 0] = remote(
            src,
            here,
            sems[13].at[j, 0, i],
            sems[14].at[j, 0, i],
            x_near if entries[j][3] else y_near,
        )

    for j in range(jobs):
        stage3(j, far - 1)
        here = place(j, z, y, x)
        for i in range(far - 1):
            hops_z[i, j] = remote(final[j], here, sems[9].at[j, i], sems[10].at[j, i], z_far[i])
        forward(j, far - 1, final[j], z)
        keep = pltpu.make_async_copy(final[j], here, sems[15].at[j])
        keep.start()
        keeps.append(keep)

    def relay(j, i, zz):
        hops1[i, j].wait_recv()
        there = place(j, zz, *((1 - y, x) if entries[j][3] else (y, 1 - x)))
        hops2[i, j, 1] = remote(
            there,
            there,
            sems[13].at[j, 1, i],
            sems[14].at[j, 1, i],
            x_near if entries[j][3] else y_near,
        )

    order = [far - 1, *range(far - 1)]
    for at_step, i in enumerate(order):
        if i < far - 1:
            zz = lax.rem(z + far - 1 - i, far)
            for j in range(jobs):
                hops_z[i, j].wait_recv()
                forward(j, i, place(j, zz, y, x), zz)
        if at_step:
            last = order[at_step - 1]
            for j in range(jobs):
                relay(j, last, lax.rem(z + 2 * far - 1 - last, far))
    for j in range(jobs):
        relay(j, order[-1], lax.rem(z + 2 * far - 1 - order[-1], far))
    for copy in hops2.values():
        copy.wait_recv()
    for keep in keeps:
        keep.wait()
    for copy in sent:
        copy.wait_send()


def reduce_all(parts):
    n_dp, n_seq = lax.axis_size("dp"), lax.axis_size("seq")
    far = n_seq // (FOLD * FOLD)
    count = len(parts)
    parts = [part.reshape(n_dp, far, FOLD, FOLD, *part.shape[2:]) for part in parts]
    entries = []
    for a, part in enumerate(parts):
        wide = part.shape[-1]
        if wide % 256:
            entries.append((a, 0, wide, True))
        else:
            entries.append((a, 0, wide // 2, True))
            entries.append((a, wide // 2, wide // 2, False))
    jobs = len(entries)
    dma = pltpu.SemaphoreType.DMA

    def slots(*lead):
        return [
            pltpu.VMEM((*lead, parts[a].shape[4], size), parts[a].dtype)
            for a, _, size, _ in entries
        ]

    results = pl.pallas_call(
        functools.partial(reduce_kernel, n_dp, n_seq, count, tuple(entries)),
        out_shape=[jax.ShapeDtypeStruct(part.shape[1:], part.dtype) for part in parts],
        in_specs=[pl.BlockSpec(memory_space=pl.ANY)] * count,
        out_specs=[pl.BlockSpec(memory_space=pl.ANY)] * count,
        scratch_shapes=(
            slots(far, FOLD, FOLD)
            + slots(n_dp - 1, far, FOLD, FOLD)
            + slots(far, FOLD)
            + slots(far, FOLD)
            + slots(far)
            + slots(far)
            + slots(far)
            + slots(far)
            + slots()
            + [dma((jobs, n_dp - 1, far))] * 2
            + [dma((jobs, far))] * 11
            + [dma((jobs, 2, far))] * 2
            + [dma((jobs,))]
        ),
        compiler_params=pltpu.CompilerParams(collective_id=0, has_side_effects=True),
        name="reduce_all",
    )(*parts)
    return [result.reshape(n_seq, *result.shape[3:]) for result in results]


TILE = 16
LANES = 128


def spread(source, target, frames, taps, skip=0):
    for shift in range(min(8, taps)):
        rows = frames + 8 * ((taps - 1 - shift) // 8)
        for s in range(source.shape[0]):
            target[shift, s, :rows, :] = source[s, skip + shift : skip + shift + rows, :]


def exchange_edges(block_ref, edges, send_sem, recv_sem):
    p, q, n_seq = lax.axis_index("dp"), lax.axis_index("seq"), lax.axis_size("seq")
    frames, border = block_ref.shape[1], edges.shape[2]
    after = (p, lax.rem(q + 1, n_seq))
    before = (p, lax.rem(q + n_seq - 1, n_seq))
    greet([after, before])
    copies = []
    for side, (start, target) in enumerate(((frames - border, after), (0, before))):
        copy = pltpu.make_async_remote_copy(
            src_ref=block_ref.at[:, pl.ds(start, border)],
            dst_ref=edges.at[side],
            send_sem=send_sem.at[side],
            recv_sem=recv_sem.at[side],
            device_id=target,
            device_id_type=MESH,
        )
        copy.start()
        copies.append(copy)
    return copies


def join_edges(block_ref, edges, full_ref, copies):
    frames, border = block_ref.shape[1], edges.shape[2]
    full_ref[:, border : border + frames, :] = block_ref[...].astype(jnp.float32)
    for copy in copies:
        copy.wait()
    full_ref[:, :border, :] = edges[0].astype(jnp.float32)
    full_ref[:, border + frames :, :] = edges[1].astype(jnp.float32)


def tap_rows(ref, s, row, k, lanes):
    start = pl.multiple_of(row + 8 * (k // 8), 8)
    return ref[k % 8, s, pl.ds(start, TILE), lanes]


def mix_kernel(
    id_ref, block_ref, tap_ref, out_ref, full_ref, ids, gated, edges, send_sem, recv_sem
):
    slabs, frames, width = out_ref.shape
    taps = tap_ref.shape[0]
    copies = exchange_edges(block_ref, edges, send_sem, recv_sem)
    spread(id_ref, ids, frames, taps)
    join_edges(block_ref, edges, full_ref, copies)
    spread(full_ref, gated, frames, taps, edges.shape[2] - taps // 2)
    every = pl.ds(0, LANES)

    @pl.loop(0, slabs)
    def _(s):
        @pl.loop(0, frames // TILE)
        def _(tile):
            row = pl.multiple_of(tile * TILE, TILE)
            center = tap_rows(ids, s, row, taps // 2, every)
            totals = [jnp.zeros((TILE, LANES), jnp.float32) for _ in range(width // LANES)]
            for k in range(taps):
                same = tap_rows(ids, s, row, k, every) == center
                for c in range(width // LANES):
                    lanes = pl.ds(c * LANES, LANES)
                    term = tap_rows(gated, s, row, k, lanes) * tap_ref[k : k + 1, lanes]
                    totals[c] = totals[c] + jnp.where(same, term, 0.0)
            for c in range(width // LANES):
                out_ref[s, pl.ds(row, TILE), pl.ds(c * LANES, LANES)] = totals[c]


def unmix_kernel(
    id_ref,
    gated_ref,
    block_ref,
    tap_ref,
    out_ref,
    tap_out_ref,
    sums,
    ids,
    gated,
    grad,
    full,
    edges,
    send_sem,
    recv_sem,
):
    slabs, frames, width = out_ref.shape
    taps = tap_ref.shape[0]
    margin = taps // 2
    copies = exchange_edges(block_ref, edges, send_sem, recv_sem)
    spread(id_ref, ids, frames, taps)
    spread(gated_ref, gated, frames, taps, edges.shape[2] - margin)
    join_edges(block_ref, edges, full, copies)
    spread(full, grad, frames, taps, edges.shape[2] - margin)
    sums[...] = jnp.zeros_like(sums)
    every = pl.ds(0, LANES)

    @pl.loop(0, slabs)
    def _(s):
        @pl.loop(0, frames // TILE)
        def _(tile):
            row = pl.multiple_of(tile * TILE, TILE)
            center = tap_rows(ids, s, row, margin, every)
            totals = [jnp.zeros((TILE, LANES), jnp.float32) for _ in range(width // LANES)]
            for k in range(taps):
                same = tap_rows(ids, s, row, k, every) == center
                mirror = taps - 1 - k
                for c in range(width // LANES):
                    lanes = pl.ds(c * LANES, LANES)
                    term = tap_rows(grad, s, row, k, lanes) * tap_ref[mirror : mirror + 1, lanes]
                    totals[c] = totals[c] + jnp.where(same, term, 0.0)
                    here = tap_rows(grad, s, row, margin, lanes)
                    cross = jnp.where(same, here * tap_rows(gated, s, row, k, lanes), 0.0)
                    folded = cross[:8]
                    for piece in range(8, TILE, 8):
                        folded = folded + cross[piece : piece + 8]
                    sums[k, :, lanes] = sums[k, :, lanes] + folded
            for c in range(width // LANES):
                out_ref[s, pl.ds(row, TILE), pl.ds(c * LANES, LANES)] = totals[c]

    for k in range(taps):
        tap_out_ref[k : k + 1, :] = jnp.sum(sums[k], axis=0, keepdims=True)


def conv_call(kernel, channel, out_shape, scratch, *args):
    whole = pl.BlockSpec(memory_space=pltpu.VMEM)
    dma = pltpu.SemaphoreType.DMA
    return pl.pallas_call(
        kernel,
        out_shape=out_shape,
        in_specs=[whole] * len(args),
        out_specs=[whole] * len(out_shape),
        scratch_shapes=[*scratch, dma((2,)), dma((2,))],
        compiler_params=pltpu.CompilerParams(collective_id=channel, has_side_effects=True),
    )(*args)


def norm_rows(values, gain):
    average = jnp.mean(values, axis=-1, keepdims=True)
    centered = values - average
    spread = jnp.mean(centered * centered, axis=-1, keepdims=True)
    return centered * lax.rsqrt(spread + 1e-05) * gain


def mid_section(values, gain):
    normed = norm_rows(values, gain)
    return normed * jax.nn.sigmoid(normed)


def per_device(
    loaded, plan, segment_ids, in_weight, out_weight, depth_kernel, norm_gains, upstream
):
    rows_dev, width = loaded.shape
    devices = plan.shape[0]
    capacity = 2 * rows_dev // devices
    slabs, slab_len = segment_ids.shape
    frames_dev = slab_len // lax.axis_size("seq")
    kernel_len = depth_kernel.shape[1]
    margin = kernel_len // 2
    sender = lax.axis_index(("dp", "seq"))
    send_plan = lax.dynamic_index_in_dim(plan, sender, 0, keepdims=False)
    send_start = jnp.cumsum(send_plan) - send_plan
    slot_index = jnp.arange(capacity, dtype=jnp.int32)
    source_rows = send_start[:, None] + slot_index[None, :]
    filled = slot_index[None, :] < send_plan[:, None]
    picked = jnp.take(loaded, jnp.clip(source_rows, 0, rows_dev - 1).reshape(-1), axis=0)
    outgoing = jnp.where(filled.reshape(-1, 1), picked, jnp.zeros_like(picked)).reshape(
        devices, capacity, width
    )
    arrived = lax.all_to_all(
        outgoing, ("dp", "seq"), split_axis=0, concat_axis=0, tiled=True
    ).reshape(devices * capacity, width)
    recv_plan = lax.dynamic_index_in_dim(plan, sender, 1, keepdims=False)
    recv_end = jnp.cumsum(recv_plan)
    frame_index = jnp.arange(rows_dev, dtype=jnp.int32)
    before = recv_end[None, :] <= frame_index[:, None]
    source_dev = jnp.sum(before.astype(jnp.int32), axis=1)
    start_of = jnp.sum(jnp.where(before, recv_plan[None, :], 0), axis=1)
    frames = jnp.take(arrived, source_dev * capacity + frame_index - start_of, axis=0)
    kernel_full, gains_full = (
        lax.all_gather(depth_kernel, "dp", axis=0, tiled=True),
        lax.all_gather(norm_gains, "dp", axis=0, tiled=True),
    )
    taps = kernel_full.astype(jnp.float32)
    gain_pre = gains_full[:, 0].astype(jnp.float32)
    gain_mid = gains_full[:, 1].astype(jnp.float32)
    frame_rows = frames.astype(jnp.float32)
    normed_full, pull_pre = jax.vjp(norm_rows, frame_rows, gain_pre)
    normed = normed_full.astype(jnp.bfloat16)
    whole_in, whole_out = (
        lax.all_gather(in_weight, "dp", axis=0, tiled=True),
        lax.all_gather(out_weight, "dp", axis=0, tiled=True),
    )
    hidden = jnp.dot(normed, whole_in, preferred_element_type=jnp.float32)
    gate_lin = hidden[:, :width]
    gate_sig = jax.nn.sigmoid(hidden[:, width:])
    gated = (gate_lin * gate_sig).astype(jnp.bfloat16).reshape(slabs, frames_dev, width)
    id_pad = jnp.pad(segment_ids, ((0, 0), (margin, margin)), constant_values=-1)
    window = lax.dynamic_slice_in_dim(
        id_pad, lax.axis_index("seq") * frames_dev, frames_dev + 2 * margin, 1
    )
    ids = jnp.broadcast_to(window[:, :, None], (*window.shape, LANES))
    taps = taps.T
    reach = frames_dev + 8 * ((kernel_len - 1) // 8)
    spread_ids = pltpu.VMEM((8, slabs, reach, LANES), jnp.int32)
    spread_rows = pltpu.VMEM((8, slabs, reach, width), jnp.float32)
    border = -(-margin // 16) * 16
    cells = jax.ShapeDtypeStruct((slabs, frames_dev, width), jnp.float32)
    longer = (slabs, frames_dev + 2 * border, width)
    mixing, gated_rows = conv_call(
        mix_kernel,
        1,
        (cells, jax.ShapeDtypeStruct(longer, jnp.float32)),
        [spread_ids, spread_rows, pltpu.VMEM((2, slabs, border, width), jnp.bfloat16)],
        ids,
        gated,
        taps,
    )
    activated_full, pull_mid = jax.vjp(mid_section, mixing.reshape(rows_dev, width), gain_mid)
    activated = activated_full.astype(jnp.bfloat16)
    upstream_rows = upstream.reshape(rows_dev, width)
    projected = jnp.dot(activated, whole_out, preferred_element_type=jnp.float32)
    grad_act = jnp.dot(upstream_rows, whole_out.T, preferred_element_type=jnp.float32)
    encoded = (frame_rows + projected).astype(jnp.bfloat16).reshape(slabs, frames_dev, width)
    grad_out_w = jnp.dot(activated.T, upstream_rows, preferred_element_type=jnp.float32)
    grad_mixing, grad_gain_mid = pull_mid(grad_act)
    grad_cells = grad_mixing.reshape(slabs, frames_dev, width)
    grad_gated, grad_taps = conv_call(
        unmix_kernel,
        2,
        (cells, jax.ShapeDtypeStruct((kernel_len, width), jnp.float32)),
        [
            pltpu.VMEM((kernel_len, 8, width), jnp.float32),
            spread_ids,
            spread_rows,
            spread_rows,
            pltpu.VMEM(longer, jnp.float32),
            pltpu.VMEM((2, slabs, border, width), jnp.float32),
        ],
        ids,
        gated_rows,
        grad_cells,
        taps,
    )
    grad_gated = grad_gated.reshape(rows_dev, width)
    grad_hidden = jnp.concatenate(
        [grad_gated * gate_sig, grad_gated * gate_lin * gate_sig * (1.0 - gate_sig)], axis=1
    ).astype(jnp.bfloat16)
    grad_in_w = jnp.dot(normed.T, grad_hidden, preferred_element_type=jnp.float32)
    grad_normed = jnp.dot(grad_hidden, whole_in.T, preferred_element_type=jnp.float32)
    grad_rows, grad_gain_pre = pull_pre(grad_normed)
    grad_frames = (
        (upstream_rows.astype(jnp.float32) + grad_rows)
        .astype(jnp.bfloat16)
        .reshape(slabs, frames_dev, width)
    )
    n_dp, n_seq = lax.axis_size("dp"), lax.axis_size("seq")
    held = width // n_dp
    piece = held // n_seq
    smalls = jnp.concatenate([grad_taps, grad_gain_pre[None], grad_gain_mid[None]], axis=0)
    lines = smalls.shape[0]
    per_dev = lines * held // n_seq
    small_rows = -(-per_dev // 1024) * 8
    smalls = smalls.reshape(lines, n_dp, held).transpose(1, 0, 2).reshape(n_dp, n_seq, per_dev)
    smalls = jnp.pad(smalls, ((0, 0), (0, 0), (0, small_rows * 128 - per_dev)))
    sum_in, sum_out, sum_small = reduce_all(
        (
            grad_in_w.astype(jnp.bfloat16).reshape(n_dp, n_seq, piece, 2 * width),
            grad_out_w.astype(jnp.bfloat16).reshape(n_dp, n_seq, piece, width),
            smalls.reshape(n_dp, n_seq, small_rows, 128),
        )
    )
    scale = 1.0 / math.sqrt(n_dp * n_seq * rows_dev)
    small = sum_small.reshape(n_seq, -1)[:, :per_dev].reshape(lines, held).T * scale
    return (
        encoded,
        grad_frames,
        sum_in.reshape(held, 2 * width).astype(jnp.float32) * scale,
        sum_out.reshape(held, width).astype(jnp.float32) * scale,
        small[:, :kernel_len],
        small[:, kernel_len:],
    )


def solution(mesh):
    placed = (
        P(("dp", "seq"), None),
        P(),
        P("dp", None),
        P("dp", None),
        P("dp", None),
        P("dp", None),
        P("dp", None),
        P("dp", "seq", None),
    )
    return jax.shard_map(
        per_device,
        mesh=mesh,
        in_specs=placed,
        out_specs=(
            P("dp", "seq", None),
            P("dp", "seq", None),
            P("dp", None),
            P("dp", None),
            P("dp", None),
            P("dp", None),
        ),
        check_vma=False,
    )
```
